128 devices in a mesh: section: 4 (over x), dp: 16 (over z, y), mp: 2 (over core).
Axes of the slice: x: 4, y: 4, z: 4, core: 2. Of those that a mesh axis runs over, the one named last changes fastest.
Arguments:
- activations: bfloat16 [4, 3, 3072, 2048], P('section', None, 'dp'), may hold values from -6 to 6
- out_grad: bfloat16 [3, 3072, 2048], P(None, 'dp'), may hold values from -6 to 6
- weight_in: bfloat16 [4, 2048, 4096], P('section', 'dp', 'mp'), may hold values from -0.125 to 0.125
- weight_out: bfloat16 [4, 4096, 2048], P('section', 'mp', 'dp'), may hold values from -0.09375 to 0.09375
- lengths: int32 [3, 16], P(None, 'dp'), may hold values from 48 to 192, as said below
Outputs:
- input_grads: bfloat16 [4, 3, 3072, 2048], P('section', None, 'dp', 'mp')
- grad_weight_in: bfloat16 [4, 2048, 4096], P('section', 'dp', 'mp')
- grad_weight_out: bfloat16 [4, 4096, 2048], P('section', 'mp', 'dp')
The draws below stay inside these ranges and needn't reach their ends.
Inputs may be any that keep to these rules, and one draw needn't show every extreme that they name: `lengths`: some replica holds a full micro-batch of 192 live tokens in every draw.
All inputs are finite; a program needn't handle non-finite values.
Results may differ from the reference program's by a relative error of at most 0.0095.
Values may be sent and summed in bfloat16 or wider, within the bound.
No kernel may reach another device: no remote copies, remote signals or barrier semaphores. Data moves between devices by JAX's collectives and lax.ppermute only.
A program may use at most 192 MiB of HBM per device.

```python
import jax
import jax.numpy as jnp

D = 2048
FFW = 4096
MB = 3
ROWS = 192
TOKENS = 3072
N_SECTION = 4
N_DP = 16


def draw_lengths(key, part):
    base = jax.random.randint(key, (MB, N_DP), ROWS // 4, ROWS + 1)
    picked = jax.random.randint(jax.random.fold_in(key, 7), (), 0, MB)
    column = jax.random.randint(jax.random.fold_in(key, 11), (), 0, N_DP)
    return base.at[picked, column].set(ROWS).astype(jnp.int32)


def shard_levels(key, shape, split, least, largest):
    level = 1.0
    for position, parts in split:
        heights = jax.random.uniform(jax.random.fold_in(jax.random.fold_in(key, 6), position), (parts,), jnp.float32, least / len(split), largest / len(split))
        level = level * jnp.repeat(jnp.exp(heights), shape[position] // parts).reshape((-1,) + (1,) * (len(shape) - 1 - position))
    return level


def bell_draw(own_key, extent, width, limit, shards=(), held_as=jnp.bfloat16):
    values = jax.random.normal(own_key, extent, jnp.float32) * width
    if len(shards) > 0:
        values = shard_levels(own_key, extent, shards, -0.22, 0.18) * values
    return jnp.clip(values, min=-limit, max=limit).astype(held_as)


def setup_inputs(seed: int = 0) -> dict:
    arg_keys = jax.random.split(jax.random.key(seed), 6)
    activations = bell_draw(arg_keys[0], (N_SECTION, MB, TOKENS, D), 1.0, 6.0, ((0, 4), (2, 16)))
    out_grad = bell_draw(arg_keys[1], (MB, TOKENS, D), 1.0, 6.0, ((1, 16),))
    weight_in = bell_draw(arg_keys[2], (N_SECTION, D, FFW), D ** -0.5, 0.125, ((0, 4), (1, 16), (2, 2)))
    weight_out = bell_draw(arg_keys[3], (N_SECTION, FFW, D), FFW ** -0.5, 0.09375, ((0, 4), (1, 2), (2, 16)))
    lengths = draw_lengths(jax.random.fold_in(arg_keys[5], 71), 0)
    return dict(activations=activations, out_grad=out_grad, weight_in=weight_in, weight_out=weight_out, lengths=lengths)


def reference(activations, out_grad, weight_in, weight_out, lengths):
    limits = jnp.repeat(lengths, ROWS, axis=1)
    valid = (jnp.arange(TOKENS)[None, :] % ROWS) < limits
    grad = jnp.where(valid[..., None], out_grad, jnp.zeros_like(out_grad)).reshape(-1, D)
    grads_list = []
    dw_in_list = []
    dw_out_list = []
    for section_index in range(N_SECTION - 1, -1, -1):
        inputs = activations[section_index].reshape(-1, D)
        pre = jnp.dot(inputs, weight_in[section_index], preferred_element_type=jnp.float32)
        sigma = jax.nn.sigmoid(pre)
        act = (pre * sigma).astype(jnp.bfloat16)
        grad_act = jnp.dot(grad, weight_out[section_index].T, preferred_element_type=jnp.float32)
        dpre = (grad_act * sigma * (1.0 + pre * (1.0 - sigma))).astype(jnp.bfloat16)
        back = jnp.dot(dpre, weight_in[section_index].T, preferred_element_type=jnp.float32)
        dw_in_list.append(jnp.dot(inputs.T, dpre, preferred_element_type=jnp.float32).astype(jnp.bfloat16))
        dw_out_list.append(jnp.dot(act.T, grad, preferred_element_type=jnp.float32).astype(jnp.bfloat16))
        grad = (grad.astype(jnp.float32) + back).astype(jnp.bfloat16)
        grads_list.append(grad.reshape(MB, TOKENS, D))
    input_grads = jnp.stack(grads_list[::-1])
    grad_weight_in = jnp.stack(dw_in_list[::-1])
    grad_weight_out = jnp.stack(dw_out_list[::-1])
    return input_grads, grad_weight_in, grad_weight_out
```

```python
import jax
import jax.numpy as jnp
from jax import lax
from jax.sharding import PartitionSpec as P

HOP = 2


def cross(left, right):
    return lax.dot_general(
        left, right, (((0,), (0,)), ((), ())), preferred_element_type=jnp.float32
    )


def times_transposed(left, right):
    return lax.dot_general(
        left, right, (((1,), (1,)), ((), ())), preferred_element_type=jnp.float32
    )


def local(activations, out_grad, weight_in, weight_out, lengths):
    sections = lax.axis_size("section")
    section_index = lax.axis_index("section")
    mp_index = lax.axis_index("mp")
    micro_count, row_count, width = out_grad.shape
    half = width // 2
    hidden_width = weight_in.shape[2]
    swap = [(0, 1), (1, 0)]
    full_in = lax.all_gather(weight_in[0], "dp", axis=0, tiled=True)
    full_out = lax.all_gather(weight_out[0], "dp", axis=1, tiled=True)
    valid = jnp.arange(row_count)[None, :] < lengths
    out_slice = lax.dynamic_slice_in_dim(out_grad, mp_index * half, half, 2)
    masked_slice = jnp.where(valid[..., None], out_slice, jnp.zeros_like(out_slice))
    saved = activations[0]

    pre = jnp.dot(saved.reshape(-1, width), full_in, preferred_element_type=jnp.float32)
    sigma = jax.nn.sigmoid(pre)
    act = (pre * sigma).astype(jnp.bfloat16)
    slope = (sigma * (1.0 + pre * (1.0 - sigma))).reshape(micro_count, row_count, hidden_width)

    depth = sections - 1 - section_index
    clocks = HOP * (sections - 1) + micro_count
    in_flight = {}
    own_list, full_list, dpre_list, result_list = [], [], [], []
    rows_other = lax.dynamic_slice_in_dim(full_in, (1 - mp_index) * half, half, 0)
    rows_own = lax.dynamic_slice_in_dim(full_in, mp_index * half, half, 0)
    for clock in range(clocks):
        micro = jnp.clip(clock - HOP * depth, 0, micro_count - 1)
        own = masked_slice[min(clock, micro_count - 1)]
        if clock in in_flight:
            own = jnp.where(section_index == sections - 1, own, in_flight.pop(clock))
        other = lax.ppermute(own, "mp", swap)
        grad_full = jnp.where(
            mp_index == 0,
            jnp.concatenate([own, other], axis=1),
            jnp.concatenate([other, own], axis=1),
        )
        grad_act = times_transposed(grad_full, full_out)
        dpre = (grad_act * lax.dynamic_index_in_dim(slope, micro, 0, keepdims=False)).astype(
            jnp.bfloat16
        )
        away = times_transposed(dpre, rows_other).astype(jnp.bfloat16)
        back = lax.ppermute(away, "mp", swap)
        kept = times_transposed(dpre, rows_own)
        result = (own.astype(jnp.float32) + (kept + back.astype(jnp.float32))).astype(jnp.bfloat16)
        full_list.append(grad_full)
        dpre_list.append(dpre)
        result_list.append(result)
        pairs = [
            (sections - 1 - k, sections - 2 - k)
            for k in range(sections - 1)
            if HOP * k <= clock < HOP * k + micro_count
        ]
        if pairs:
            in_flight[clock + HOP] = lax.ppermute(result, "section", pairs)

    def window(parts):
        stacked = jnp.stack(parts)
        return lax.dynamic_slice_in_dim(stacked, HOP * depth, micro_count, 0)

    grads = window(result_list)
    grad_flat = window(full_list).reshape(-1, width)
    dh_flat = window(dpre_list).reshape(-1, hidden_width)
    part_out = cross(act, grad_flat).astype(jnp.bfloat16)
    dw_out = lax.psum_scatter(part_out, "dp", scatter_dimension=1, tiled=True)
    part_in = cross(saved.reshape(-1, width), dh_flat).astype(jnp.bfloat16)
    dw_in = lax.psum_scatter(part_in, "dp", scatter_dimension=0, tiled=True)
    return (grads[None], dw_in[None], dw_out[None])


def solution(mesh):
    return jax.shard_map(
        local,
        mesh=mesh,
        in_specs=(
            P("section", None, "dp", None),
            P(None, "dp", None),
            P("section", "dp", "mp"),
            P("section", "mp", "dp"),
            P(None, "dp"),
        ),
        out_specs=(
            P("section", None, "dp", "mp"),
            P("section", "dp", "mp"),
            P("section", "mp", "dp"),
        ),
        check_vma=False,
    )
```

```python
import functools

import jax
import jax.numpy as jnp
from jax import lax
from jax.experimental import pallas as pl
from jax.experimental.pallas import tpu as pltpu
from jax.sharding import PartitionSpec as P

HOP = 2
SIDE = 4
GRANT = 58 * 2**20
BF16 = jnp.bfloat16
F32 = jnp.float32


def moved(x, axis, by):
    pairs = []
    for z in range(SIDE):
        for y in range(SIDE):
            to = (z, (y + by) % SIDE) if axis == "y" else ((z + by) % SIDE, y)
            pairs.append((z * SIDE + y, to[0] * SIDE + to[1]))
    return lax.ppermute(x, "dp", pairs)


def gathered(x, axis):
    cut = x.shape[0] // 2
    before = moved(x, axis, 1)
    after = moved(x, axis, -1)
    far_low = moved(before[:cut], axis, 1)
    far_high = moved(after[cut:], axis, -1)
    return x, before, after, far_low, far_high


def gather_weight(shard, z, y):
    rows, cols = shard.shape
    half = cols // 2
    full = jnp.zeros((SIDE, SIDE, rows, cols), shard.dtype)
    for colour, (first, second) in enumerate((("y", "z"), ("z", "y"))):
        here, there = (y, z) if first == "y" else (z, y)
        own = shard[:, colour * half : (colour + 1) * half]
        own, before, after, low, high = gathered(own, first)
        group = jnp.zeros((SIDE, rows, half), shard.dtype)
        opposite = (here + 2) % SIDE
        for part, at, row in (
            (own, here, 0),
            (before, (here + SIDE - 1) % SIDE, 0),
            (after, (here + 1) % SIDE, 0),
            (low, opposite, 0),
            (high, opposite, rows // 2),
        ):
            group = lax.dynamic_update_slice(group, part[None], (at, row, 0))
        own, before, after, low, high = gathered(group, second)
        opposite = (there + 2) % SIDE
        for part, at, row in (
            (own, there, 0),
            (before, (there + SIDE - 1) % SIDE, 0),
            (after, (there + 1) % SIDE, 0),
            (low, opposite, 0),
            (high, opposite, SIDE // 2),
        ):
            if second == "z":
                full = lax.dynamic_update_slice(full, part[None], (at, row, 0, colour * half))
            else:
                full = lax.dynamic_update_slice(full, part[:, None], (row, at, 0, colour * half))
    return full.reshape(SIDE * SIDE * rows, cols)


def summed(block, axis):
    opposite = block(2)
    cut = opposite.shape[0] // 2
    low = moved(opposite[:cut].astype(BF16), axis, 1)
    high = moved(opposite[cut:].astype(BF16), axis, -1)
    ahead = block(1)
    ahead = jnp.concatenate([(ahead[:cut].astype(F32) + low.astype(F32)).astype(BF16), ahead[cut:].astype(BF16)])
    behind = block(3)
    behind = jnp.concatenate([behind[:cut].astype(BF16), (behind[cut:].astype(F32) + high.astype(F32)).astype(BF16)])
    from_before = moved(ahead, axis, 1)
    from_after = moved(behind, axis, -1)
    return block(0).astype(F32) + (from_before.astype(F32) + from_after.astype(F32))


def scatter_sum(terms, z, y):
    rows, cols = terms.shape[0] // (SIDE * SIDE), terms.shape[1]
    half = cols // 2
    grid = terms.reshape(SIDE, SIDE, rows, cols)
    sums = []
    for colour, (first, second) in enumerate((("z", "y"), ("y", "z"))):
        here, there = (y, z) if first == "y" else (z, y)

        def big(k):
            at = (here + k) % SIDE
            if first == "z":
                return lax.dynamic_slice(
                    grid, (at, 0, 0, colour * half), (1, SIDE, rows, half)
                )[0]
            return lax.dynamic_slice(
                grid, (0, at, 0, colour * half), (SIDE, 1, rows, half)
            )[:, 0]

        group = summed(big, first)
        sums.append(
            summed(
                lambda k: lax.dynamic_index_in_dim(group, (there + k) % SIDE, 0, keepdims=False),
                second,
            )
        )
    return jnp.concatenate(sums, axis=1).astype(BF16)


def product_kernel(a_ref, b_ref, out_ref):
    out_ref[...] = lax.dot_general(
        a_ref[...], b_ref[...], (((0,), (0,)), ((), ())), preferred_element_type=F32
    ).astype(out_ref.dtype)


def cross(a, b):
    depth, rows = a.shape
    cols = b.shape[1]
    tile_r, tile_c = 512, 1024
    return pl.pallas_call(
        product_kernel,
        out_shape=jax.ShapeDtypeStruct((rows, cols), BF16),
        grid=(rows // tile_r, cols // tile_c),
        in_specs=[
            pl.BlockSpec((depth, tile_r), lambda i, j: (0, i)),
            pl.BlockSpec((depth, tile_c), lambda i, j: (0, j)),
        ],
        out_specs=pl.BlockSpec((tile_r, tile_c), lambda i, j: (i, j)),
        compiler_params=pltpu.CompilerParams(vmem_limit_bytes=24 * 2**20),
        cost_estimate=pl.CostEstimate(
            flops=2 * depth * rows * cols,
            bytes_accessed=2 * (depth * (rows + cols) + rows * cols),
            transcendentals=0,
        ),
        name="cross",
    )(a, b)


def step_kernel(steps, info, own, other, slope, w_out, w_in, full, dpre, away):
    i = pl.program_id(0)
    half = own.shape[1]

    @pl.when((i == 0) & (info[0] == 0))
    def _():
        full[:, :half] = own[...]
        full[:, half:] = other[...]

    @pl.when((i == 0) & (info[0] == 1))
    def _():
        full[:, :half] = other[...]
        full[:, half:] = own[...]

    @pl.when(i < steps)
    def _():
        width = w_out.shape[0]
        grad_act = lax.dot_general(
            full[...], w_out[...], (((1,), (1,)), ((), ())), preferred_element_type=F32
        )
        at = pl.ds(pl.multiple_of(i * width, width), width)
        dpre[:, at] = (grad_act * slope[0]).astype(BF16)

    @pl.when(i >= steps)
    def _():
        away[...] = lax.dot_general(
            dpre[...], w_in[...], (((1,), (1,)), ((), ())), preferred_element_type=F32
        ).astype(BF16)


def relay_step(info, own, other, slopes, w_out, w_in):
    rows, half = own.shape
    hidden, width = w_out.shape
    steps = 4
    tile_h, tile_d = hidden // steps, half // steps
    first = lambda i: jnp.minimum(i, steps - 1)
    later = lambda i: jnp.maximum(i - steps, 0)
    return pl.pallas_call(
        functools.partial(step_kernel, steps),
        out_shape=(
            jax.ShapeDtypeStruct((rows, width), BF16),
            jax.ShapeDtypeStruct((rows, hidden), BF16),
            jax.ShapeDtypeStruct((rows, half), BF16),
        ),
        grid_spec=pltpu.PrefetchScalarGridSpec(
            num_scalar_prefetch=1,
            grid=(2 * steps,),
            in_specs=[
                pl.BlockSpec((rows, half), lambda i, s: (0, 0)),
                pl.BlockSpec((rows, half), lambda i, s: (0, 0)),
                pl.BlockSpec((1, rows, tile_h), lambda i, s: (s[1], 0, first(i))),
                pl.BlockSpec((tile_h, width), lambda i, s: (first(i), 0)),
                pl.BlockSpec((tile_d, hidden), lambda i, s: ((1 - s[0]) * steps + later(i), 0)),
            ],
            out_specs=[
                pl.BlockSpec((rows, width), lambda i, s: (0, 0)),
                pl.BlockSpec((rows, hidden), lambda i, s: (0, 0)),
                pl.BlockSpec((rows, tile_d), lambda i, s: (0, later(i))),
            ],
        ),
        compiler_params=pltpu.CompilerParams(vmem_limit_bytes=GRANT),
        cost_estimate=pl.CostEstimate(
            flops=2 * rows * hidden * (width + half),
            bytes_accessed=2 * hidden * (width + half) + 8 * rows * width,
            transcendentals=0,
        ),
        name="relay_step",
    )(info, own, other, slopes, w_out, w_in)


def kept_kernel(info, own, dpre, w_in, out):
    out[...] = own[...].astype(F32) + lax.dot_general(
        dpre[...], w_in[...], (((1,), (1,)), ((), ())), preferred_element_type=F32
    )


def kept_half(info, own, dpre, w_in):
    rows, half = own.shape
    hidden = dpre.shape[1]
    steps = 4
    tile_d = half // steps
    return pl.pallas_call(
        kept_kernel,
        out_shape=jax.ShapeDtypeStruct((rows, half), F32),
        grid_spec=pltpu.PrefetchScalarGridSpec(
            num_scalar_prefetch=1,
            grid=(steps,),
            in_specs=[
                pl.BlockSpec((rows, tile_d), lambda i, s: (0, i)),
                pl.BlockSpec((rows, hidden), lambda i, s: (0, 0)),
                pl.BlockSpec((tile_d, hidden), lambda i, s: (s[0] * steps + i, 0)),
            ],
            out_specs=pl.BlockSpec((rows, tile_d), lambda i, s: (0, i)),
        ),
        compiler_params=pltpu.CompilerParams(vmem_limit_bytes=GRANT),
        cost_estimate=pl.CostEstimate(
            flops=2 * rows * hidden * half,
            bytes_accessed=2 * hidden * half + 6 * rows * half,
            transcendentals=0,
        ),
        name="kept_half",
    )(info, own, dpre, w_in)


def local(activations, out_grad, weight_in, weight_out, lengths):
    sections = lax.axis_size("section")
    section_index = lax.axis_index("section")
    mp_index = lax.axis_index("mp")
    dp_index = lax.axis_index("dp")
    z, y = dp_index // SIDE, dp_index % SIDE
    micro_count, row_count, width = out_grad.shape
    half = width // 2
    hidden_width = weight_in.shape[2]
    swap = [(0, 1), (1, 0)]
    full_out = lax.all_gather(weight_out[0], "dp", axis=1, tiled=True)
    full_in = gather_weight(weight_in[0], z, y)
    valid = jnp.arange(row_count)[None, :] < lengths
    out_slice = lax.dynamic_slice_in_dim(out_grad, mp_index * half, half, 2)
    masked_slice = jnp.where(valid[..., None], out_slice, jnp.zeros_like(out_slice))
    saved = activations[0]

    acts, slopes = [], []
    for micro in range(micro_count):
        pre = jnp.dot(saved[micro], full_in, preferred_element_type=F32)
        sigma = jax.nn.sigmoid(pre)
        acts.append((pre * sigma).astype(BF16))
        slopes.append(sigma * (1.0 + pre * (1.0 - sigma)))
    all_slopes = jnp.stack(slopes)

    depth = sections - 1 - section_index
    clocks = HOP * (sections - 1) + micro_count
    in_flight = {}
    full_list, dpre_list, result_list = [], [], []
    for clock in range(clocks):
        possible = [clock - HOP * k for k in range(sections) if 0 <= clock - HOP * k < micro_count]
        if len(possible) == 1:
            these, micro = slopes[possible[0]][None], jnp.int32(0)
        else:
            these, micro = all_slopes, jnp.clip(clock - HOP * depth, 0, micro_count - 1)
        info = jnp.stack([mp_index, micro]).astype(jnp.int32)
        own = masked_slice[min(clock, micro_count - 1)]
        if clock in in_flight:
            own = jnp.where(section_index == sections - 1, own, in_flight.pop(clock))
        other = lax.ppermute(own, "mp", swap)
        grad_full, dpre, away = relay_step(info, own, other, these, full_out, full_in)
        back = lax.ppermute(away, "mp", swap)
        kept = kept_half(info, own, dpre, full_in)
        result = (kept + back.astype(F32)).astype(BF16)
        full_list.append(grad_full)
        dpre_list.append(dpre)
        result_list.append(result)
        pairs = [
            (sections - 1 - k, sections - 2 - k)
            for k in range(sections - 1)
            if HOP * k <= clock < HOP * k + micro_count
        ]
        if pairs:
            in_flight[clock + HOP] = lax.ppermute(result, "section", pairs)

    def window(parts):
        picked = []
        for micro in range(micro_count):
            value = parts[micro]
            for k in range(1, sections):
                value = jnp.where(depth == k, parts[micro + HOP * k], value)
            picked.append(value)
        return picked

    grads = jnp.stack(window(result_list))
    grad_flat = jnp.concatenate(window(full_list))
    part_out = cross(grad_flat, jnp.concatenate(acts))
    dw_out = lax.psum_scatter(part_out, "dp", scatter_dimension=0, tiled=True).T
    dh_flat = jnp.concatenate(window(dpre_list))
    part_in = cross(saved.reshape(-1, width), dh_flat)
    dw_in = scatter_sum(part_in, z, y)
    return (grads[None], dw_in[None], dw_out[None])


def solution(mesh):
    return jax.shard_map(
        local,
        mesh=mesh,
        in_specs=(
            P("section", None, "dp", None),
            P(None, "dp", None),
            P("section", "dp", "mp"),
            P("section", "mp", "dp"),
            P(None, "dp"),
        ),
        out_specs=(
            P("section", None, "dp", "mp"),
            P("section", "dp", "mp"),
            P("section", "mp", "dp"),
        ),
        check_vma=False,
    )
```

```python
import functools

import jax
import jax.numpy as jnp
from jax import lax
from jax.experimental import pallas as pl
from jax.experimental.pallas import tpu as pltpu
from jax.sharding import PartitionSpec as P

HOP = 2
SIDE = 4
GRANT = 56 * 2**20
BF16 = jnp.bfloat16
F32 = jnp.float32


def moved(x, axis, by):
    pairs = []
    for z in range(SIDE):
        for y in range(SIDE):
            to = (z, (y + by) % SIDE) if axis == "y" else ((z + by) % SIDE, y)
            pairs.append((z * SIDE + y, to[0] * SIDE + to[1]))
    return lax.ppermute(x, "dp", pairs)


def gathered(x, axis):
    cut = x.shape[0] // 2
    before = moved(x, axis, 1)
    after = moved(x, axis, -1)
    far_low = moved(before[:cut], axis, 1)
    far_high = moved(after[cut:], axis, -1)
    return x, before, after, far_low, far_high


def gather_weight(shard, z, y):
    rows, cols = shard.shape
    half = cols // 2
    full = jnp.zeros((SIDE, SIDE, rows, cols), shard.dtype)
    for colour, (first, second) in enumerate((("y", "z"), ("z", "y"))):
        here, there = (y, z) if first == "y" else (z, y)
        own = shard[:, colour * half : (colour + 1) * half]
        own, before, after, low, high = gathered(own, first)
        group = jnp.zeros((SIDE, rows, half), shard.dtype)
        opposite = (here + 2) % SIDE
        for part, at, row in (
            (own, here, 0),
            (before, (here + SIDE - 1) % SIDE, 0),
            (after, (here + 1) % SIDE, 0),
            (low, opposite, 0),
            (high, opposite, rows // 2),
        ):
            group = lax.dynamic_update_slice(group, part[None], (at, row, 0))
        own, before, after, low, high = gathered(group, second)
        opposite = (there + 2) % SIDE
        for part, at, row in (
            (own, there, 0),
            (before, (there + SIDE - 1) % SIDE, 0),
            (after, (there + 1) % SIDE, 0),
            (low, opposite, 0),
            (high, opposite, SIDE // 2),
        ):
            if second == "z":
                full = lax.dynamic_update_slice(full, part[None], (at, row, 0, colour * half))
            else:
                full = lax.dynamic_update_slice(full, part[:, None], (row, at, 0, colour * half))
    return full.reshape(SIDE * SIDE * rows, cols)


def summed(block, axis):
    opposite = block(2)
    cut = opposite.shape[0] // 2
    low = moved(opposite[:cut].astype(BF16), axis, 1)
    high = moved(opposite[cut:].astype(BF16), axis, -1)
    ahead = block(1)
    ahead = jnp.concatenate([(ahead[:cut].astype(F32) + low.astype(F32)).astype(BF16), ahead[cut:].astype(BF16)])
    behind = block(3)
    behind = jnp.concatenate([behind[:cut].astype(BF16), (behind[cut:].astype(F32) + high.astype(F32)).astype(BF16)])
    from_before = moved(ahead, axis, 1)
    from_after = moved(behind, axis, -1)
    return block(0).astype(F32) + (from_before.astype(F32) + from_after.astype(F32))


def scatter_sum(terms, z, y):
    rows, cols = terms.shape[0] // (SIDE * SIDE), terms.shape[1]
    half = cols // 2
    grid = terms.reshape(SIDE, SIDE, rows, cols)
    sums = []
    for colour, (first, second) in enumerate((("z", "y"), ("y", "z"))):
        here, there = (y, z) if first == "y" else (z, y)

        def big(k):
            at = (here + k) % SIDE
            if first == "z":
                return lax.dynamic_slice(
                    grid, (at, 0, 0, colour * half), (1, SIDE, rows, half)
                )[0]
            return lax.dynamic_slice(
                grid, (0, at, 0, colour * half), (SIDE, 1, rows, half)
            )[:, 0]

        group = summed(big, first)
        sums.append(
            summed(
                lambda k: lax.dynamic_index_in_dim(group, (there + k) % SIDE, 0, keepdims=False),
                second,
            )
        )
    return jnp.concatenate(sums, axis=1).astype(BF16)


def product_kernel(a_ref, b_ref, out_ref):
    out_ref[...] = lax.dot_general(
        a_ref[...], b_ref[...], (((0,), (0,)), ((), ())), preferred_element_type=F32
    ).astype(out_ref.dtype)


def cross(a, b):
    depth, rows = a.shape
    cols = b.shape[1]
    tile_r, tile_c = 512, 1024
    return pl.pallas_call(
        product_kernel,
        out_shape=jax.ShapeDtypeStruct((rows, cols), BF16),
        grid=(rows // tile_r, cols // tile_c),
        in_specs=[
            pl.BlockSpec((depth, tile_r), lambda i, j: (0, i)),
            pl.BlockSpec((depth, tile_c), lambda i, j: (0, j)),
        ],
        out_specs=pl.BlockSpec((tile_r, tile_c), lambda i, j: (i, j)),
        compiler_params=pltpu.CompilerParams(vmem_limit_bytes=24 * 2**20),
        cost_estimate=pl.CostEstimate(
            flops=2 * depth * rows * cols,
            bytes_accessed=2 * (depth * (rows + cols) + rows * cols),
            transcendentals=0,
        ),
        name="cross",
    )(a, b)


CHUNKS = 4


def step_kernel(info, own, other, slopes, w_out, w_in, full, dpre, away, kept, slope, wo, wi, sems):
    half = own.shape[1]
    hidden = w_out.shape[0]
    tile = hidden // CHUNKS
    each = CHUNKS // 2
    copies = []
    for i in range(CHUNKS):
        source = w_out.at[pl.ds(i * tile, tile), :]
        copies.append(pltpu.make_async_copy(source, wo.at[i], sems.at[i]))
    copies.append(pltpu.make_async_copy(slopes.at[info[1]], slope, sems.at[2 * CHUNKS]))
    for i in range(CHUNKS):
        side = 1 - info[0] if i < each else info[0]
        start = pl.multiple_of(side * half + (i % each) * tile, tile)
        source = w_in.at[pl.ds(start, tile), :]
        copies.append(pltpu.make_async_copy(source, wi.at[i], sems.at[CHUNKS + i]))
    for copy in copies:
        copy.start()

    @pl.when(info[0] == 0)
    def _():
        full[:, :half] = own[...]
        full[:, half:] = other[...]

    @pl.when(info[0] == 1)
    def _():
        full[:, :half] = other[...]
        full[:, half:] = own[...]

    copies[CHUNKS].wait()
    for i in range(CHUNKS):
        copies[i].wait()
        at = slice(i * tile, (i + 1) * tile)
        grad_act = lax.dot_general(
            full[...], wo[i], (((1,), (1,)), ((), ())), preferred_element_type=F32
        )
        dpre[:, at] = (grad_act * slope[:, at]).astype(BF16)
    for i in range(CHUNKS):
        copies[CHUNKS + 1 + i].wait()
        part = lax.dot_general(
            dpre[...], wi[i], (((1,), (1,)), ((), ())), preferred_element_type=F32
        )
        at = slice((i % each) * tile, (i % each + 1) * tile)
        if i < each:
            away[:, at] = part.astype(BF16)
        else:
            kept[:, at] = own[:, at].astype(F32) + part


VMEM = pl.BlockSpec(memory_space=pltpu.VMEM)
SMEM = pl.BlockSpec(memory_space=pltpu.SMEM)
ANY = pl.BlockSpec(memory_space=pl.ANY)


def relay_step(info, own, other, slopes, w_out, w_in):
    rows, half = own.shape
    hidden, width = w_out.shape
    tile = hidden // CHUNKS
    return pl.pallas_call(
        step_kernel,
        out_shape=(
            jax.ShapeDtypeStruct((rows, width), BF16),
            jax.ShapeDtypeStruct((rows, hidden), BF16),
            jax.ShapeDtypeStruct((rows, half), BF16),
            jax.ShapeDtypeStruct((rows, half), F32),
        ),
        in_specs=[SMEM, VMEM, VMEM, ANY, ANY, ANY],
        out_specs=[VMEM] * 4,
        scratch_shapes=[
            pltpu.VMEM((rows, hidden), F32),
            pltpu.VMEM((CHUNKS, tile, width), BF16),
            pltpu.VMEM((CHUNKS, tile, hidden), BF16),
            pltpu.SemaphoreType.DMA((2 * CHUNKS + 1,)),
        ],
        compiler_params=pltpu.CompilerParams(vmem_limit_bytes=GRANT),
        cost_estimate=pl.CostEstimate(
            flops=4 * rows * hidden * width,
            bytes_accessed=4 * hidden * width + 12 * rows * width,
            transcendentals=0,
        ),
        name="relay_step",
    )(info, own, other, slopes, w_out, w_in)


def local(activations, out_grad, weight_in, weight_out, lengths):
    sections = lax.axis_size("section")
    section_index = lax.axis_index("section")
    mp_index = lax.axis_index("mp")
    dp_index = lax.axis_index("dp")
    z, y = dp_index // SIDE, dp_index % SIDE
    micro_count, row_count, width = out_grad.shape
    half = width // 2
    hidden_width = weight_in.shape[2]
    swap = [(0, 1), (1, 0)]
    full_out = lax.all_gather(weight_out[0], "dp", axis=1, tiled=True)
    full_in = gather_weight(weight_in[0], z, y)
    valid = jnp.arange(row_count)[None, :] < lengths
    out_slice = lax.dynamic_slice_in_dim(out_grad, mp_index * half, half, 2)
    masked_slice = jnp.where(valid[..., None], out_slice, jnp.zeros_like(out_slice))
    saved = activations[0]

    pre = jnp.dot(saved.reshape(-1, width), full_in, preferred_element_type=F32)
    sigma = jax.nn.sigmoid(pre)
    act = (pre * sigma).astype(BF16)
    slopes = (sigma * (1.0 + pre * (1.0 - sigma))).reshape(micro_count, row_count, hidden_width)

    depth = sections - 1 - section_index
    clocks = HOP * (sections - 1) + micro_count
    in_flight = {}
    full_list, dpre_list, result_list = [], [], []
    for clock in range(clocks):
        micro = jnp.clip(clock - HOP * depth, 0, micro_count - 1)
        info = jnp.stack([mp_index, micro]).astype(jnp.int32)
        own = masked_slice[min(clock, micro_count - 1)]
        if clock in in_flight:
            incoming, full_list[-1] = lax.optimization_barrier((in_flight.pop(clock), full_list[-1]))
            own = jnp.where(section_index == sections - 1, own, incoming)
        other = lax.ppermute(own, "mp", swap)
        if result_list:
            other, result_list[-1] = lax.optimization_barrier((other, result_list[-1]))
        grad_full, dpre, away, kept = relay_step(info, own, other, slopes, full_out, full_in)
        back = lax.ppermute(away, "mp", swap)
        result = (kept + back.astype(F32)).astype(BF16)
        full_list.append(grad_full)
        dpre_list.append(dpre)
        result_list.append(result)
        pairs = [
            (sections - 1 - k, sections - 2 - k)
            for k in range(sections - 1)
            if HOP * k <= clock < HOP * k + micro_count
        ]
        if pairs:
            in_flight[clock + HOP] = lax.ppermute(result, "section", pairs)

    def window(parts):
        picked = []
        for micro in range(micro_count):
            value = parts[micro]
            for k in range(1, sections):
                value = jnp.where(depth == k, parts[micro + HOP * k], value)
            picked.append(value)
        return picked

    grads = jnp.stack(window(result_list))
    grad_flat = jnp.concatenate(window(full_list))
    part_out = cross(grad_flat, act)
    dw_out = lax.psum_scatter(part_out, "dp", scatter_dimension=0, tiled=True).T
    dh_flat = jnp.concatenate(window(dpre_list))
    part_in = cross(saved.reshape(-1, width), dh_flat)
    dw_in = scatter_sum(part_in, z, y)
    return (grads[None], dw_in[None], dw_out[None])


def solution(mesh):
    return jax.shard_map(
        local,
        mesh=mesh,
        in_specs=(
            P("section", None, "dp", None),
            P(None, "dp", None),
            P("section", "dp", "mp"),
            P("section", "mp", "dp"),
            P(None, "dp"),
        ),
        out_specs=(
            P("section", None, "dp", "mp"),
            P("section", "dp", "mp"),
            P("section", "mp", "dp"),
        ),
        check_vma=False,
    )
```

```python
import functools

import jax
import jax.numpy as jnp
from jax import lax
from jax.experimental import pallas as pl
from jax.experimental.pallas import tpu as pltpu
from jax.sharding import PartitionSpec as P

HOP = 2
SIDE = 4
GRANT = 56 * 2**20
BF16 = jnp.bfloat16
F32 = jnp.float32


def moved(x, axis, by):
    pairs = []
    for z in range(SIDE):
        for y in range(SIDE):
            to = (z, (y + by) % SIDE) if axis == "y" else ((z + by) % SIDE, y)
            pairs.append((z * SIDE + y, to[0] * SIDE + to[1]))
    return lax.ppermute(x, "dp", pairs)


def gathered(x, axis):
    cut = x.shape[0] // 2
    before = moved(x, axis, 1)
    after = moved(x, axis, -1)
    far_low = moved(before[:cut], axis, 1)
    far_high = moved(after[cut:], axis, -1)
    return x, before, after, far_low, far_high


def gather_weight(shard, z, y):
    rows, cols = shard.shape
    half = cols // 2
    full = jnp.zeros((SIDE, SIDE, rows, cols), shard.dtype)
    for colour, (first, second) in enumerate((("y", "z"), ("z", "y"))):
        here, there = (y, z) if first == "y" else (z, y)
        own = shard[:, colour * half : (colour + 1) * half]
        own, before, after, low, high = gathered(own, first)
        group = jnp.zeros((SIDE, rows, half), shard.dtype)
        opposite = (here + 2) % SIDE
        for part, at, row in (
            (own, here, 0),
            (before, (here + SIDE - 1) % SIDE, 0),
            (after, (here + 1) % SIDE, 0),
            (low, opposite, 0),
            (high, opposite, rows // 2),
        ):
            group = lax.dynamic_update_slice(group, part[None], (at, row, 0))
        own, before, after, low, high = gathered(group, second)
        opposite = (there + 2) % SIDE
        for part, at, row in (
            (own, there, 0),
            (before, (there + SIDE - 1) % SIDE, 0),
            (after, (there + 1) % SIDE, 0),
            (low, opposite, 0),
            (high, opposite, SIDE // 2),
        ):
            if second == "z":
                full = lax.dynamic_update_slice(full, part[None], (at, row, 0, colour * half))
            else:
                full = lax.dynamic_update_slice(full, part[:, None], (row, at, 0, colour * half))
    return full.reshape(SIDE * SIDE * rows, cols)


def summed(block, axis):
    opposite = block(2)
    cut = opposite.shape[0] // 2
    low = moved(opposite[:cut].astype(BF16), axis, 1)
    high = moved(opposite[cut:].astype(BF16), axis, -1)
    ahead = block(1)
    ahead = jnp.concatenate([(ahead[:cut].astype(F32) + low.astype(F32)).astype(BF16), ahead[cut:].astype(BF16)])
    behind = block(3)
    behind = jnp.concatenate([behind[:cut].astype(BF16), (behind[cut:].astype(F32) + high.astype(F32)).astype(BF16)])
    from_before = moved(ahead, axis, 1)
    from_after = moved(behind, axis, -1)
    return block(0).astype(F32) + (from_before.astype(F32) + from_after.astype(F32))


def scatter_sum(terms, z, y):
    rows, cols = terms.shape[0] // (SIDE * SIDE), terms.shape[1]
    half = cols // 2
    grid = terms.reshape(SIDE, SIDE, rows, cols)
    sums = []
    for colour, (first, second) in enumerate((("z", "y"), ("y", "z"))):
        here, there = (y, z) if first == "y" else (z, y)

        def big(k):
            at = (here + k) % SIDE
            if first == "z":
                return lax.dynamic_slice(
                    grid, (at, 0, 0, colour * half), (1, SIDE, rows, half)
                )[0]
            return lax.dynamic_slice(
                grid, (0, at, 0, colour * half), (SIDE, 1, rows, half)
            )[:, 0]

        group = summed(big, first)
        sums.append(
            summed(
                lambda k: lax.dynamic_index_in_dim(group, (there + k) % SIDE, 0, keepdims=False),
                second,
            )
        )
    return jnp.concatenate(sums, axis=1).astype(BF16)


def product_kernel(a_ref, b_ref, out_ref):
    out_ref[...] = lax.dot_general(
        a_ref[...], b_ref[...], (((0,), (0,)), ((), ())), preferred_element_type=F32
    ).astype(out_ref.dtype)


def cross(a, b):
    depth, rows = a.shape
    cols = b.shape[1]
    tile_r, tile_c = 512, 1024
    return pl.pallas_call(
        product_kernel,
        out_shape=jax.ShapeDtypeStruct((rows, cols), BF16),
        grid=(rows // tile_r, cols // tile_c),
        in_specs=[
            pl.BlockSpec((depth, tile_r), lambda i, j: (0, i)),
            pl.BlockSpec((depth, tile_c), lambda i, j: (0, j)),
        ],
        out_specs=pl.BlockSpec((tile_r, tile_c), lambda i, j: (i, j)),
        compiler_params=pltpu.CompilerParams(vmem_limit_bytes=GRANT),
        cost_estimate=pl.CostEstimate(
            flops=2 * depth * rows * cols,
            bytes_accessed=2 * (depth * (rows + cols) + rows * cols),
            transcendentals=0,
        ),
        name="cross",
    )(a, b)


CHUNKS = 2
AHEAD = 2


def step_kernel(info, own, other, slopes, w_out, w_in, full, dpre, away, kept, slope, wo, wi, sems):
    half = own.shape[1]
    hidden = w_out.shape[0]
    tile = hidden // CHUNKS
    each = CHUNKS // 2
    copies = [pltpu.make_async_copy(slopes.at[info[1]], slope, sems.at[2 * CHUNKS])]
    for i in range(CHUNKS):
        source = w_out.at[pl.ds(i * tile, tile), :]
        copies.append(pltpu.make_async_copy(source, wo.at[i], sems.at[i]))
    for i in range(CHUNKS):
        side = 1 - info[0] if i < each else info[0]
        start = pl.multiple_of(side * half + (i % each) * tile, tile)
        source = w_in.at[pl.ds(start, tile), :]
        copies.append(pltpu.make_async_copy(source, wi.at[i], sems.at[CHUNKS + i]))
    for copy in copies[:AHEAD]:
        copy.start()

    @pl.when(info[0] == 0)
    def _():
        full[:, :half] = own[...]
        full[:, half:] = other[...]

    @pl.when(info[0] == 1)
    def _():
        full[:, :half] = other[...]
        full[:, half:] = own[...]

    def arrived(n):
        copies[n].wait()
        if n + AHEAD < len(copies):
            copies[n + AHEAD].start()

    arrived(0)
    for i in range(CHUNKS):
        arrived(1 + i)
        at = slice(i * tile, (i + 1) * tile)
        grad_act = lax.dot_general(
            full[...], wo[i], (((1,), (1,)), ((), ())), preferred_element_type=F32
        )
        dpre[:, at] = (grad_act * slope[:, at]).astype(BF16)
    for i in range(CHUNKS):
        arrived(CHUNKS + 1 + i)
        part = lax.dot_general(
            dpre[...], wi[i], (((1,), (1,)), ((), ())), preferred_element_type=F32
        )
        at = slice((i % each) * tile, (i % each + 1) * tile)
        if i < each:
            away[:, at] = part.astype(BF16)
        else:
            kept[:, at] = own[:, at].astype(F32) + part


VMEM = pl.BlockSpec(memory_space=pltpu.VMEM)
SMEM = pl.BlockSpec(memory_space=pltpu.SMEM)
ANY = pl.BlockSpec(memory_space=pl.ANY)


def relay_step(info, own, other, slopes, w_out, w_in):
    rows, half = own.shape
    hidden, width = w_out.shape
    tile = hidden // CHUNKS
    return pl.pallas_call(
        step_kernel,
        out_shape=(
            jax.ShapeDtypeStruct((rows, width), BF16),
            jax.ShapeDtypeStruct((rows, hidden), BF16),
            jax.ShapeDtypeStruct((rows, half), BF16),
            jax.ShapeDtypeStruct((rows, half), F32),
        ),
        in_specs=[SMEM, VMEM, VMEM, ANY, ANY, ANY],
        out_specs=[VMEM] * 4,
        scratch_shapes=[
            pltpu.VMEM((rows, hidden), F32),
            pltpu.VMEM((CHUNKS, tile, width), BF16),
            pltpu.VMEM((CHUNKS, tile, hidden), BF16),
            pltpu.SemaphoreType.DMA((2 * CHUNKS + 1,)),
        ],
        compiler_params=pltpu.CompilerParams(vmem_limit_bytes=GRANT),
        cost_estimate=pl.CostEstimate(
            flops=4 * rows * hidden * width,
            bytes_accessed=4 * hidden * width + 12 * rows * width,
            transcendentals=0,
        ),
        name="relay_step",
    )(info, own, other, slopes, w_out, w_in)


def local(activations, out_grad, weight_in, weight_out, lengths):
    sections = lax.axis_size("section")
    section_index = lax.axis_index("section")
    mp_index = lax.axis_index("mp")
    dp_index = lax.axis_index("dp")
    z, y = dp_index // SIDE, dp_index % SIDE
    micro_count, row_count, width = out_grad.shape
    half = width // 2
    hidden_width = weight_in.shape[2]
    swap = [(0, 1), (1, 0)]
    full_out = lax.all_gather(weight_out[0], "dp", axis=1, tiled=True)
    full_in = gather_weight(weight_in[0], z, y)
    valid = jnp.arange(row_count)[None, :] < lengths
    out_slice = lax.dynamic_slice_in_dim(out_grad, mp_index * half, half, 2)
    masked_slice = jnp.where(valid[..., None], out_slice, jnp.zeros_like(out_slice))
    saved = activations[0]

    pre = jnp.dot(saved.reshape(-1, width), full_in, preferred_element_type=F32)
    sigma = jax.nn.sigmoid(pre)
    act = (pre * sigma).astype(BF16)
    slopes = (sigma * (1.0 + pre * (1.0 - sigma))).reshape(micro_count, row_count, hidden_width)

    depth = sections - 1 - section_index
    clocks = HOP * (sections - 1) + micro_count
    in_flight = {}
    full_list, dpre_list, result_list = [], [], []
    for clock in range(clocks):
        micro = jnp.clip(clock - HOP * depth, 0, micro_count - 1)
        info = jnp.stack([mp_index, micro]).astype(jnp.int32)
        own = masked_slice[min(clock, micro_count - 1)]
        if clock in in_flight:
            incoming, full_list[-1] = lax.optimization_barrier((in_flight.pop(clock), full_list[-1]))
            own = jnp.where(section_index == sections - 1, own, incoming)
        other = lax.ppermute(own, "mp", swap)
        if result_list:
            other, result_list[-1] = lax.optimization_barrier((other, result_list[-1]))
        grad_full, dpre, away, kept = relay_step(info, own, other, slopes, full_out, full_in)
        back = lax.ppermute(away, "mp", swap)
        result = (kept + back.astype(F32)).astype(BF16)
        full_list.append(grad_full)
        dpre_list.append(dpre)
        result_list.append(result)
        pairs = [
            (sections - 1 - k, sections - 2 - k)
            for k in range(sections - 1)
            if HOP * k <= clock < HOP * k + micro_count
        ]
        if pairs:
            in_flight[clock + HOP] = lax.ppermute(result, "section", pairs)

    def window(parts):
        picked = []
        for micro in range(micro_count):
            value = parts[micro]
            for k in range(1, sections):
                value = jnp.where(depth == k, parts[micro + HOP * k], value)
            picked.append(value)
        return picked

    grads = jnp.stack(window(result_list))
    grad_flat = jnp.concatenate(window(full_list))
    part_out = cross(grad_flat, act)
    dw_out = lax.psum_scatter(part_out, "dp", scatter_dimension=0, tiled=True).T
    dh_flat = jnp.concatenate(window(dpre_list))
    part_in = cross(saved.reshape(-1, width), dh_flat)
    dw_in = scatter_sum(part_in, z, y)
    return (grads[None], dw_in[None], dw_out[None])


def solution(mesh):
    return jax.shard_map(
        local,
        mesh=mesh,
        in_specs=(
            P("section", None, "dp", None),
            P(None, "dp", None),
            P("section", "dp", "mp"),
            P("section", "mp", "dp"),
            P(None, "dp"),
        ),
        out_specs=(
            P("section", None, "dp", "mp"),
            P("section", "dp", "mp"),
            P("section", "mp", "dp"),
        ),
        check_vma=False,
    )
```
